32 devices in a mesh: groups: 2 (over y), row: 4 (over z), col: 4 (over x, core).
Axes of the slice: x: 2, y: 2, z: 4, core: 2. Of those that a mesh axis runs over, the one named last changes fastest.
Arguments:
- right_side: float32 [128, 8192], P('groups', ('row', 'col')), parts along dimension 0, may hold values from -6 to 6
- prior: float32 [8192], P(('row', 'col')), may hold values from 0.5 to 2
- blocks: bfloat16 [1024, 128, 128], P(('row', 'col')), may hold values from -0.125 to 0.125
- block_row: int32 [1024], P(('row', 'col')), may hold values from 0 to 63, as said below
- block_col: int32 [1024], P(('row', 'col')), may hold values from 0 to 63, as said below
Outputs:
- solution_field: float32 [128, 8192], P('groups', ('row', 'col')), parts along dimension 0
- residual: float32 [128, 8192], P('groups', ('row', 'col')), parts along dimension 0
The draws below stay inside these ranges and needn't reach their ends.
There are 2 independent parts, one for each index of `groups`. The reference program is written for one: setup_inputs(seed, part) draws one part's arguments, and reference() takes and returns one part's arrays. A program takes and returns all parts, laid end to end along the dimension named above; an argument that names none is the same for every part. Nothing has to cross between parts.
Inputs may be any that keep to these rules, and one draw needn't show every extreme that they name: `block_row`: stored blocks k*64 to (k+1)*64 - 1 belong to device k of row+col, k = r*4+c; their block rows lie in r*16 to (r+1)*16 - 1. `block_col`: the block columns b of device (r, c) satisfy (b // 4) % 4 == c.
All inputs are finite; a program needn't handle non-finite values.
Results may differ from the reference program's by a relative error of at most 0.0069.
Values may be sent and summed in bfloat16 or wider, within the bound.
A program may use at most 64 MiB of HBM per device.

```python
import math
import jax
import jax.numpy as jnp
from jax import lax

BLOCK = 128
FRAMES = 64
CB = 4
KB = 64
ITERS = 2
GRID_ROWS = 4
GRID_COLS = 4
ROWBLK = 16
NBLK = 64
NPIX = 8192
NNZ = 1024


def draw_block_row(key, part):
    device = jnp.arange(NNZ, dtype=jnp.int32) // KB
    position = jnp.arange(NNZ, dtype=jnp.int32) % KB
    grid_row = device // GRID_COLS
    offset_row = jax.random.randint(jax.random.fold_in(key, 11), (NNZ,), 0, ROWBLK, dtype=jnp.int32)
    offset_row = jnp.where(position == 0, 0, offset_row)
    offset_row = jnp.where(position == KB - 1, ROWBLK - 1, offset_row)
    return (grid_row * ROWBLK + offset_row).astype(jnp.int32)


def draw_block_col(key, part):
    key_stretch, key_inner = jax.random.split(jax.random.fold_in(key, 23))
    device = jnp.arange(NNZ, dtype=jnp.int32) // KB
    position = jnp.arange(NNZ, dtype=jnp.int32) % KB
    grid_col = device % GRID_COLS
    stretch_row = jax.random.randint(key_stretch, (NNZ,), 0, GRID_ROWS, dtype=jnp.int32)
    inner = jax.random.randint(key_inner, (NNZ,), 0, CB, dtype=jnp.int32)
    stretch_row = jnp.where(position == 0, 0, stretch_row)
    inner = jnp.where(position == 0, 0, inner)
    stretch_row = jnp.where(position == KB - 1, GRID_ROWS - 1, stretch_row)
    inner = jnp.where(position == KB - 1, CB - 1, inner)
    return ((stretch_row * GRID_COLS + grid_col) * CB + inner).astype(jnp.int32)


def block_scale(own_key, shape, cuts, low, high):
    factor_of = 1.0
    for axis_at, shards_of in cuts:
        heights = jax.random.uniform(jax.random.fold_in(jax.random.fold_in(own_key, 6), axis_at), (shards_of,), jnp.float32, low / len(cuts), high / len(cuts))
        factor_of = factor_of * jnp.repeat(jnp.exp(heights), shape[axis_at] // shards_of).reshape((-1,) + (1,) * (len(shape) - 1 - axis_at))
    return factor_of


def bell_draw(own_key, shape, scale, bound, pieces=(), kind=jnp.bfloat16):
    values = scale * jax.random.normal(own_key, shape, jnp.float32)
    if pieces:
        values = values * block_scale(own_key, shape, pieces, -0.22, 0.18)
    return jnp.clip(values, -bound, bound).astype(kind)


def setup_inputs(seed: int = 0, part: int = 0) -> dict:
    arg_keys = jax.random.split(jax.random.key(seed), 6)
    part_splits = jax.random.split(jax.random.fold_in(arg_keys[5], part), 6)
    return {
        "right_side": bell_draw(part_splits[0], (FRAMES, NPIX), 1.0, 6.0, ((1, 16),), jnp.float32),
        "prior": jnp.clip(jnp.exp(math.log(2.0) - 1.3862944 * jax.random.uniform(arg_keys[1], (NPIX,), jnp.float32) ** block_scale(arg_keys[1], (NPIX,), ((0, 16),), -0.2, 0.2)), 0.5, 2.0),
        "blocks": bell_draw(arg_keys[2], (NNZ, BLOCK, BLOCK), (KB // CB * BLOCK) ** -0.5, 0.125, ((0, 16),)),
        "block_row": draw_block_row(jax.random.fold_in(arg_keys[5], 71), part),
        "block_col": draw_block_col(jax.random.fold_in(arg_keys[5], 71), part),
    }


def spd_solve(matrix, rhs):
    factor = jnp.linalg.cholesky(matrix)
    half_solved = lax.linalg.triangular_solve(factor, rhs, left_side=True, lower=True)
    return lax.linalg.triangular_solve(factor, half_solved, left_side=True, lower=True, transpose_a=True)

def pair_gram(left, right):
    return lax.dot_general(left.astype(jnp.float32), right.astype(jnp.float32), (((1,), (1,)), ((), ())), precision=lax.Precision.HIGHEST, preferred_element_type=jnp.float32)

def apply_left(coeffs, panel):
    return jnp.dot(coeffs.astype(jnp.float32), panel.astype(jnp.float32), precision=lax.Precision.HIGHEST, preferred_element_type=jnp.float32)

def operator(grouped, prior, direction):
    search = direction.astype(jnp.bfloat16).astype(jnp.float32)
    panel_view = search.reshape(FRAMES, NBLK, BLOCK)

    def forward_step(total, stacked):
        tile_set, row_ids, col_ids = stacked
        picked = jnp.take(panel_view, col_ids, axis=1)
        contrib = jnp.einsum('fkj,kij->kfi', picked, tile_set.astype(jnp.float32), precision=lax.Precision.HIGHEST)
        return (total.at[row_ids].add(contrib), None)
    total, _ = lax.scan(forward_step, jnp.zeros((NBLK, FRAMES, BLOCK), jnp.float32), grouped)
    footprint = total.transpose(1, 0, 2).reshape(FRAMES, NPIX).astype(jnp.bfloat16).astype(jnp.float32)
    foot_view = footprint.reshape(FRAMES, NBLK, BLOCK)

    def backward_step(total, stacked):
        tile_set, row_ids, col_ids = stacked
        picked = jnp.take(foot_view, row_ids, axis=1)
        contrib = jnp.einsum('fki,kij->kfj', picked, tile_set.astype(jnp.float32), precision=lax.Precision.HIGHEST)
        return (total.at[col_ids].add(contrib), None)
    total, _ = lax.scan(backward_step, jnp.zeros((NBLK, FRAMES, BLOCK), jnp.float32), grouped)
    return total.transpose(1, 0, 2).reshape(FRAMES, NPIX) + prior[None, :] * direction

def reference(right_side, prior, blocks, block_row, block_col):
    devices = GRID_ROWS * GRID_COLS
    grouped = (blocks.reshape(devices, KB, BLOCK, BLOCK), block_row.reshape(devices, KB).astype(jnp.int32), block_col.reshape(devices, KB).astype(jnp.int32))
    solution = jnp.zeros_like(right_side)
    residual = right_side
    direction = right_side
    gram = pair_gram(residual, residual)
    for iteration in range(ITERS):
        image = operator(grouped, prior, direction)
        curvature = pair_gram(direction, image)
        step_alpha = spd_solve(curvature, gram)
        solution = solution + apply_left(step_alpha.T, direction)
        residual = residual - apply_left(step_alpha.T, image)
        if iteration + 1 < ITERS:
            new_gram = pair_gram(residual, residual)
            step_beta = spd_solve(gram, new_gram)
            direction = residual + apply_left(step_beta.T, direction)
            gram = new_gram
    return (solution, residual)
```

```python
import functools

import jax
import jax.numpy as jnp
from jax import lax
from jax.experimental import pallas as pl
from jax.experimental.pallas import tpu as pltpu
from jax.sharding import PartitionSpec as P

BLOCK = 128
ITERS = 2
UNROLL = 8
MESH = pl.DeviceIdType.MESH
HIGHEST = lax.Precision.HIGHEST
f32 = jnp.float32
bf16 = jnp.bfloat16


def dot(left, right, dims):
    return lax.dot_general(
        left, right, (dims, ((), ())), precision=HIGHEST, preferred_element_type=f32
    )


def pair_gram(left, right):
    return dot(left, right, ((1,), (1,)))


def left_t(coeffs, panel):
    return dot(coeffs, panel, ((0,), (0,)))


def gauss_jordan(aug, frames):
    rows = lax.broadcasted_iota(jnp.int32, aug.shape, 0)
    for j in range(frames):
        at = frames + j
        lead = aug[j : j + 1, :] * (1.0 / aug[j : j + 1, at : at + 1])
        aug = jnp.where(rows == j, lead, aug - aug[:, at : at + 1] * lead)
    return aug[:, :frames]


def kernel(
    nr, nc, cb, kb, frames,
    tab, keep, rhs_ref, prior_ref, blocks_hbm, sol_ref, res_ref,
    blocks, panel, foot, sendf, sendb, landf, landb, scan, image, direct, aug,
    gc0, gr0, gc1, gr1, gc2, gr2,
    blk_sem, ag_s, ag_r, rs_s, rs_r, fg_s, fg_r, br_s, br_r, gc_s, gc_r, gr_s, gr_r,
):
    r = lax.axis_index("row")
    c = lax.axis_index("col")
    nrow, ncol = cb * nc, cb * nr
    half = frames // 2
    pending = []

    load = pltpu.make_async_copy(blocks_hbm, blocks, blk_sem)
    load.start()

    barrier = pltpu.get_barrier_semaphore()
    for axis, me, n in (("row", r, nr), ("col", c, nc)):
        for o in range(1, n):
            pl.semaphore_signal(
                barrier, inc=1, device_id={axis: lax.rem(me + o, n)}, device_id_type=MESH
            )

    def send(axis, me, n, src, dst, ssem, rsem):
        copies = []
        for o in range(1, n):
            peer = lax.rem(me + o, n)
            copy = pltpu.make_async_remote_copy(
                src_ref=src(peer), dst_ref=dst(o), send_sem=ssem.at[o - 1],
                recv_sem=rsem.at[o - 1], device_id={axis: peer}, device_id_type=MESH,
            )
            copy.start()
            copies.append(copy)
        pending.extend(copies)
        return copies

    def arrive(copies):
        for copy in copies:
            copy.wait_recv()

    def share(axis, me, n, buf, ssem, rsem, width=1):
        at = lambda _: buf.at[pl.ds(me * width, width)]
        return send(axis, me, n, at, at, ssem, rsem)

    def total(buf, n):
        out = buf[0]
        for i in range(1, n):
            out = out + buf[i]
        return out

    def fold(buf, me, gram):
        buf[me, :, :frames] = gram[:half]
        buf[me, :, frames:] = gram[half:]

    def unfold(packed):
        return jnp.concatenate([packed[:, :frames], packed[:, frames:]], axis=0)

    def put_panel(it, value):
        for b in range(cb):
            panel[it, r * cb + b] = value[:, b * BLOCK : (b + 1) * BLOCK].astype(bf16)

    def gather_rows(it):
        return share("row", r, nr, panel.at[it], ag_s.at[it], ag_r.at[it], cb)

    def sweep(source, it, order_at, keep_at, side):
        def body(q, run):
            for u in range(UNROLL):
                t = q * UNROLL + u
                run = run * keep[keep_at + t] + lax.dot_general(
                    source[it, tab[order_at + kb + t]],
                    blocks[tab[order_at + t]],
                    (((1,), (side,)), ((), ())),
                    preferred_element_type=f32,
                )
                scan[t] = run
            return run

        lax.fori_loop(0, kb // UNROLL, body, jnp.zeros((frames, BLOCK), f32))

    def segment(end_at, valid_at, i):
        return scan[tab[end_at + i]] * keep[valid_at + i]

    tab_c = 2 * kb + nrow
    keep_c = kb + nrow

    rhs = rhs_ref[...]
    put_panel(0, rhs)
    fold(gc0, c, pair_gram(rhs, rhs))
    pl.semaphore_wait(barrier, nr + nc - 2)

    gather = gather_rows(0)
    gram_cols = share("col", c, nc, gc0, gc_s.at[0], gc_r.at[0])
    residual = rhs_ref
    gram = None
    for it in range(ITERS):
        last = it + 1 == ITERS
        now = rhs_ref if it == 0 else direct
        if it == 0:
            load.wait()
        arrive(gather)
        sweep(panel, it, 0, 0, 1)
        for i in range(nrow):
            sendf[it, i] = segment(2 * kb, kb, i).astype(bf16)
        copies = send(
            "col", c, nc,
            lambda p: sendf.at[it, pl.ds(p * cb, cb)], lambda o: landf.at[it, o - 1],
            rs_s.at[it], rs_r.at[it],
        )
        if it == 0:
            arrive(gram_cols)
            gr0[r] = total(gc0, nc)
            gram_rows = share("row", r, nr, gr0, gr_s.at[0], gr_r.at[0])
        arrive(copies)
        for b in range(cb):
            own = segment(2 * kb, kb, c * cb + b)
            for o in range(1, nc):
                own = own + landf[it, o - 1, b].astype(f32)
            foot[it, c * cb + b] = own.astype(bf16)
        copies = share("col", c, nc, foot.at[it], fg_s.at[it], fg_r.at[it], cb)
        if it == 0:
            arrive(gram_rows)
            gram = unfold(total(gr0, nr))
            aug[:, frames:] = gram
            eye = lax.broadcasted_iota(jnp.int32, (frames, frames), 0)
            aug[:, :frames] = (
                eye == lax.broadcasted_iota(jnp.int32, (frames, frames), 1)
            ).astype(f32)
            gram_inverse = gauss_jordan(aug[...], frames)
        arrive(copies)
        sweep(foot, it, tab_c, keep_c, 0)
        for i in range(ncol):
            sendb[it, i] = segment(tab_c + 2 * kb, keep_c + kb, i).astype(bf16)
        copies = send(
            "row", r, nr,
            lambda p: sendb.at[it, pl.ds(p * cb, cb)], lambda o: landb.at[it, o - 1],
            br_s.at[it], br_r.at[it],
        )
        arrive(copies)
        for b in range(cb):
            at = slice(b * BLOCK, (b + 1) * BLOCK)
            own = segment(tab_c + 2 * kb, keep_c + kb, r * cb + b)
            for o in range(1, nr):
                own = own + landb[it, o - 1, b].astype(f32)
            image[:, at] = own + prior_ref[:, at] * now[:, at]
        direction = now[...]
        im = image[...]
        curvature = pair_gram(direction, im)
        if last:
            fold(gc2, c, curvature)
            cols, rows = gc2, gr2
        else:
            gc1[c, :, :frames] = curvature
            gc1[c, :, frames:] = pair_gram(im, im)
            cols, rows = gc1, gr1
        arrive(share("col", c, nc, cols, gc_s.at[it + 1], gc_r.at[it + 1]))
        rows[r] = total(cols, nc)
        arrive(share("row", r, nr, rows, gr_s.at[it + 1], gr_r.at[it + 1]))
        summed = total(rows, nr)
        curvature = unfold(summed) if last else summed[:, :frames]
        aug[:, :frames] = gram
        aug[:, frames:] = curvature
        alpha = gauss_jordan(aug[...], frames)
        new_residual = (rhs_ref if it == 0 else res_ref)[...] - left_t(alpha, im)
        res_ref[...] = new_residual
        if not last:
            image_gram = summed[:, frames:]
            mixed = dot(curvature, alpha, ((1,), (0,)))
            new_gram = (
                gram
                - mixed
                - left_t(alpha, curvature.T)
                + left_t(alpha, dot(image_gram, alpha, ((1,), (0,))))
            )
            beta = dot(gram_inverse, new_gram, ((1,), (0,)))
            direct[...] = new_residual + left_t(beta, direction)
            put_panel(it + 1, direct)
            gather = gather_rows(it + 1)
            gram = new_gram
        update = left_t(alpha, direction)
        sol_ref[...] = update if it == 0 else sol_ref[...] + update
    for copy in pending:
        copy.wait_send()


def order_by(key, other, count):
    kb = key.shape[0]
    ids = jnp.arange(kb, dtype=jnp.int32)
    full = key * kb + ids
    rank = jnp.sum((full[None, :] < full[:, None]).astype(jnp.int32), axis=1)
    onehot = (rank[None, :] == ids[:, None]).astype(jnp.int32)
    order = jnp.sum(onehot * ids[None, :], axis=1)
    picks = jnp.sum(onehot * other[None, :], axis=1)
    keys = jnp.sum(onehot * key[None, :], axis=1)
    keep = jnp.concatenate([jnp.zeros((1,), f32), (keys[1:] == keys[:-1]).astype(f32)])
    slots = jnp.arange(count, dtype=jnp.int32)[:, None]
    ends = jnp.maximum(jnp.sum((key[None, :] <= slots).astype(jnp.int32), axis=1) - 1, 0)
    valid = jnp.max((key[None, :] == slots).astype(f32), axis=1)
    return [order, picks, ends], [keep, valid]


def shards(right_side, prior, blocks, block_row, block_col):
    frames, pix = right_side.shape
    kb = blocks.shape[0]
    cb = pix // BLOCK
    nr = lax.axis_size("row")
    nc = lax.axis_size("col")
    nrow, ncol = cb * nc, cb * nr
    row_local = block_row % nrow
    col_local = block_col // nrow * cb + block_col % cb
    ints_r, keep_r = order_by(row_local, col_local, nrow)
    ints_c, keep_c = order_by(col_local, row_local, ncol)
    tab = jnp.concatenate(ints_r + ints_c)
    keep = jnp.concatenate(keep_r + keep_c)
    vm = pl.BlockSpec(memory_space=pltpu.VMEM)
    sm = pl.BlockSpec(memory_space=pltpu.SMEM)
    dma = pltpu.SemaphoreType.DMA
    tile = (frames, BLOCK)
    half = (frames // 2, 2 * frames)
    wide = (frames, 2 * frames)
    out = jax.ShapeDtypeStruct(right_side.shape, f32)
    return pl.pallas_call(
        functools.partial(kernel, nr, nc, cb, kb, frames),
        out_shape=(out, out),
        in_specs=[sm, sm, vm, vm, pl.BlockSpec(memory_space=pl.ANY)],
        out_specs=(vm, vm),
        scratch_shapes=[
            pltpu.VMEM(blocks.shape, bf16),
            pltpu.VMEM((ITERS, ncol) + tile, bf16),
            pltpu.VMEM((ITERS, nrow) + tile, bf16),
            pltpu.VMEM((ITERS, nrow) + tile, bf16),
            pltpu.VMEM((ITERS, ncol) + tile, bf16),
            pltpu.VMEM((ITERS, nc - 1, cb) + tile, bf16),
            pltpu.VMEM((ITERS, nr - 1, cb) + tile, bf16),
            pltpu.VMEM((kb,) + tile, f32),
            pltpu.VMEM(right_side.shape, f32),
            pltpu.VMEM(right_side.shape, f32),
            pltpu.VMEM(wide, f32),
            pltpu.VMEM((nc,) + half, f32),
            pltpu.VMEM((nr,) + half, f32),
            pltpu.VMEM((nc,) + wide, f32),
            pltpu.VMEM((nr,) + wide, f32),
            pltpu.VMEM((nc,) + half, f32),
            pltpu.VMEM((nr,) + half, f32),
            dma,
            dma((ITERS, nr - 1)), dma((ITERS, nr - 1)),
            dma((ITERS, nc - 1)), dma((ITERS, nc - 1)),
            dma((ITERS, nc - 1)), dma((ITERS, nc - 1)),
            dma((ITERS, nr - 1)), dma((ITERS, nr - 1)),
            dma((ITERS + 1, nc - 1)), dma((ITERS + 1, nc - 1)),
            dma((ITERS + 1, nr - 1)), dma((ITERS + 1, nr - 1)),
        ],
        compiler_params=pltpu.CompilerParams(
            collective_id=0, has_side_effects=True, vmem_limit_bytes=48 << 20
        ),
    )(tab, keep, right_side, prior[None, :], blocks)


def solution(mesh):
    return jax.shard_map(
        shards,
        mesh=mesh,
        in_specs=(
            P("groups", ("row", "col")),
            P(("row", "col")),
            P(("row", "col"), None, None),
            P(("row", "col")),
            P(("row", "col")),
        ),
        out_specs=(P("groups", ("row", "col")), P("groups", ("row", "col"))),
        check_vma=False,
    )
```

```python
import functools

import jax
import jax.numpy as jnp
from jax import lax
from jax.experimental import pallas as pl
from jax.experimental.pallas import tpu as pltpu
from jax.sharding import PartitionSpec as P

BLOCK = 128
ITERS = 2
UNROLL = 8
MESH = pl.DeviceIdType.MESH
HIGHEST = lax.Precision.HIGHEST
f32 = jnp.float32
bf16 = jnp.bfloat16


def dot(left, right, dims):
    return lax.dot_general(
        left, right, (dims, ((), ())), precision=HIGHEST, preferred_element_type=f32
    )


def pair_gram(left, right):
    return dot(left, right, ((1,), (1,)))


def left_t(coeffs, panel):
    return dot(coeffs, panel, ((0,), (0,)))


def gauss_jordan(aug, frames):
    rows = lax.broadcasted_iota(jnp.int32, aug.shape, 0)
    for j in range(frames):
        at = frames + j
        lead = aug[j : j + 1, :] * (1.0 / aug[j : j + 1, at : at + 1])
        aug = jnp.where(rows == j, lead, aug - aug[:, at : at + 1] * lead)
    return aug[:, :frames]


def kernel(
    nr, nc, cb, kb, frames,
    tab, keep, rhs_ref, prior_ref, blocks_hbm, sol_ref, res_ref,
    blocks, panel, foot, sendf, sendb, landf, landb, scan, image, direct, aug,
    gc0, gr0, gc1, gr1, gc2, gr2,
    blk_sem, ag_s, ag_r, rs_s, rs_r, fg_s, fg_r, br_s, br_r, gc_s, gc_r, gr_s, gr_r,
    nc_s, nc_r, nr_s, nr_r,
):
    r = lax.axis_index("row")
    c = lax.axis_index("col")
    nrow, ncol = cb * nc, cb * nr
    half = frames // 2
    pending = []

    load = pltpu.make_async_copy(blocks_hbm, blocks, blk_sem)
    load.start()

    barrier = pltpu.get_barrier_semaphore()
    for axis, me, n in (("row", r, nr), ("col", c, nc)):
        for o in range(1, n):
            pl.semaphore_signal(
                barrier, inc=1, device_id={axis: lax.rem(me + o, n)}, device_id_type=MESH
            )

    def send(axis, me, n, src, dst, ssem, rsem):
        copies = []
        for o in range(1, n):
            peer = lax.rem(me + o, n)
            copy = pltpu.make_async_remote_copy(
                src_ref=src(peer), dst_ref=dst(o), send_sem=ssem.at[o - 1],
                recv_sem=rsem.at[o - 1], device_id={axis: peer}, device_id_type=MESH,
            )
            copy.start()
            copies.append(copy)
        pending.extend(copies)
        return copies

    def arrive(copies):
        for copy in copies:
            copy.wait_recv()

    def share(axis, me, n, buf, ssem, rsem, width=1):
        at = lambda _: buf.at[pl.ds(me * width, width)]
        return send(axis, me, n, at, at, ssem, rsem)

    def total(buf, n):
        out = buf[0]
        for i in range(1, n):
            out = out + buf[i]
        return out

    def fold(buf, me, gram):
        buf[me, :, :frames] = gram[:half]
        buf[me, :, frames:] = gram[half:]

    def unfold(packed):
        return jnp.concatenate([packed[:, :frames], packed[:, frames:]], axis=0)

    def put_panel(it, value):
        for b in range(cb):
            panel[it, r * cb + b] = value[:, b * BLOCK : (b + 1) * BLOCK].astype(bf16)

    def gather_rows(it):
        return share("row", r, nr, panel.at[it], ag_s.at[it], ag_r.at[it], cb)

    def sweep(source, it, order_at, keep_at, side):
        def body(q, run):
            for u in range(UNROLL):
                t = q * UNROLL + u
                run = run * keep[keep_at + t] + lax.dot_general(
                    source[it, tab[order_at + kb + t]],
                    blocks[tab[order_at + t]],
                    (((1,), (side,)), ((), ())),
                    preferred_element_type=f32,
                )
                scan[t] = run
            return run

        lax.fori_loop(0, kb // UNROLL, body, jnp.zeros((frames, BLOCK), f32))

    def segment(end_at, valid_at, i):
        return scan[tab[end_at + i]] * keep[valid_at + i]

    tab_c = 2 * kb + nrow
    keep_c = kb + nrow

    rhs = rhs_ref[...]
    put_panel(0, rhs)
    fold(gc0, c, pair_gram(rhs, rhs))
    pl.semaphore_wait(barrier, nr + nc - 2)

    gather = gather_rows(0)
    gram_cols = share("col", c, nc, gc0, gc_s.at[0], gc_r.at[0])
    gram = None
    for it in range(ITERS):
        last = it + 1 == ITERS
        now = rhs_ref if it == 0 else direct
        if it == 0:
            load.wait()
        arrive(gather)
        sweep(panel, it, 0, 0, 1)
        for i in range(nrow):
            sendf[it, i] = segment(2 * kb, kb, i).astype(bf16)
        copies = send(
            "col", c, nc,
            lambda p: sendf.at[it, pl.ds(p * cb, cb)], lambda o: landf.at[it, o - 1],
            rs_s.at[it], rs_r.at[it],
        )
        if it == 0:
            arrive(gram_cols)
            gr0[r] = total(gc0, nc)
            gram_rows = share("row", r, nr, gr0, gr_s.at[0], gr_r.at[0])
        direction = now[...]
        curvature = pair_gram(direction, prior_ref[...] * direction)
        arrive(copies)
        for b in range(cb):
            own = segment(2 * kb, kb, c * cb + b)
            for o in range(1, nc):
                own = own + landf[it, o - 1, b].astype(f32)
            rounded = own.astype(bf16)
            foot[it, c * cb + b] = rounded
            image[:, b * BLOCK : (b + 1) * BLOCK] = own
        copies = share("col", c, nc, foot.at[it], fg_s.at[it], fg_r.at[it], cb)
        own = image[...]
        curvature = curvature + pair_gram(own, own.astype(bf16).astype(f32))
        fold(gc1.at[it], c, curvature)
        curve_cols = share("col", c, nc, gc1.at[it], gc_s.at[it + 1], gc_r.at[it + 1])
        if it == 0:
            arrive(gram_rows)
            gram = unfold(total(gr0, nr))
            aug[:, frames:] = gram
            eye = lax.broadcasted_iota(jnp.int32, (frames, frames), 0)
            aug[:, :frames] = (
                eye == lax.broadcasted_iota(jnp.int32, (frames, frames), 1)
            ).astype(f32)
            gram_inverse = gauss_jordan(aug[...], frames)
        arrive(curve_cols)
        gr1[it, r] = total(gc1.at[it], nc)
        curve_rows = share("row", r, nr, gr1.at[it], gr_s.at[it + 1], gr_r.at[it + 1])
        arrive(copies)
        sweep(foot, it, tab_c, keep_c, 0)
        for i in range(ncol):
            sendb[it, i] = segment(tab_c + 2 * kb, keep_c + kb, i).astype(bf16)
        copies = send(
            "row", r, nr,
            lambda p: sendb.at[it, pl.ds(p * cb, cb)], lambda o: landb.at[it, o - 1],
            br_s.at[it], br_r.at[it],
        )
        arrive(curve_rows)
        curvature = unfold(total(gr1.at[it], nr))
        aug[:, :frames] = gram
        aug[:, frames:] = 0.5 * (curvature + curvature.T)
        alpha = gauss_jordan(aug[...], frames)
        update = left_t(alpha, direction)
        sol_ref[...] = update if it == 0 else sol_ref[...] + update
        arrive(copies)
        for b in range(cb):
            at = slice(b * BLOCK, (b + 1) * BLOCK)
            own = segment(tab_c + 2 * kb, keep_c + kb, r * cb + b)
            for o in range(1, nr):
                own = own + landb[it, o - 1, b].astype(f32)
            image[:, at] = own + prior_ref[:, at] * now[:, at]
        residual = (rhs_ref if it == 0 else res_ref)[...] - left_t(alpha, image[...])
        res_ref[...] = residual
        if not last:
            fold(gc2.at[it], c, pair_gram(residual, residual))
            arrive(share("col", c, nc, gc2.at[it], nc_s.at[it], nc_r.at[it]))
            gr2[it, r] = total(gc2.at[it], nc)
            arrive(share("row", r, nr, gr2.at[it], nr_s.at[it], nr_r.at[it]))
            gram = unfold(total(gr2.at[it], nr))
            beta = dot(gram_inverse, gram, ((1,), (0,)))
            direct[...] = residual + left_t(beta, direction)
            put_panel(it + 1, direct)
            gather = gather_rows(it + 1)
    for copy in pending:
        copy.wait_send()


def order_by(key, other, count):
    kb = key.shape[0]
    ids = jnp.arange(kb, dtype=jnp.int32)
    full = key * kb + ids
    rank = jnp.sum((full[None, :] < full[:, None]).astype(jnp.int32), axis=1)
    onehot = (rank[None, :] == ids[:, None]).astype(jnp.int32)
    order = jnp.sum(onehot * ids[None, :], axis=1)
    picks = jnp.sum(onehot * other[None, :], axis=1)
    keys = jnp.sum(onehot * key[None, :], axis=1)
    keep = jnp.concatenate([jnp.zeros((1,), f32), (keys[1:] == keys[:-1]).astype(f32)])
    slots = jnp.arange(count, dtype=jnp.int32)[:, None]
    ends = jnp.maximum(jnp.sum((key[None, :] <= slots).astype(jnp.int32), axis=1) - 1, 0)
    valid = jnp.max((key[None, :] == slots).astype(f32), axis=1)
    return [order, picks, ends], [keep, valid]


def shards(right_side, prior, blocks, block_row, block_col):
    frames, pix = right_side.shape
    kb = blocks.shape[0]
    cb = pix // BLOCK
    nr = lax.axis_size("row")
    nc = lax.axis_size("col")
    nrow, ncol = cb * nc, cb * nr
    row_local = block_row % nrow
    col_local = block_col // nrow * cb + block_col % cb
    ints_r, keep_r = order_by(row_local, col_local, nrow)
    ints_c, keep_c = order_by(col_local, row_local, ncol)
    tab = jnp.concatenate(ints_r + ints_c)
    keep = jnp.concatenate(keep_r + keep_c)
    vm = pl.BlockSpec(memory_space=pltpu.VMEM)
    sm = pl.BlockSpec(memory_space=pltpu.SMEM)
    dma = pltpu.SemaphoreType.DMA
    tile = (frames, BLOCK)
    half = (frames // 2, 2 * frames)
    wide = (frames, 2 * frames)
    out = jax.ShapeDtypeStruct(right_side.shape, f32)
    return pl.pallas_call(
        functools.partial(kernel, nr, nc, cb, kb, frames),
        out_shape=(out, out),
        in_specs=[sm, sm, vm, vm, pl.BlockSpec(memory_space=pl.ANY)],
        out_specs=(vm, vm),
        scratch_shapes=[
            pltpu.VMEM(blocks.shape, bf16),
            pltpu.VMEM((ITERS, ncol) + tile, bf16),
            pltpu.VMEM((ITERS, nrow) + tile, bf16),
            pltpu.VMEM((ITERS, nrow) + tile, bf16),
            pltpu.VMEM((ITERS, ncol) + tile, bf16),
            pltpu.VMEM((ITERS, nc - 1, cb) + tile, bf16),
            pltpu.VMEM((ITERS, nr - 1, cb) + tile, bf16),
            pltpu.VMEM((kb,) + tile, f32),
            pltpu.VMEM(right_side.shape, f32),
            pltpu.VMEM(right_side.shape, f32),
            pltpu.VMEM(wide, f32),
            pltpu.VMEM((nc,) + half, f32),
            pltpu.VMEM((nr,) + half, f32),
            pltpu.VMEM((ITERS, nc) + half, f32),
            pltpu.VMEM((ITERS, nr) + half, f32),
            pltpu.VMEM((ITERS - 1, nc) + half, f32),
            pltpu.VMEM((ITERS - 1, nr) + half, f32),
            dma,
            dma((ITERS, nr - 1)), dma((ITERS, nr - 1)),
            dma((ITERS, nc - 1)), dma((ITERS, nc - 1)),
            dma((ITERS, nc - 1)), dma((ITERS, nc - 1)),
            dma((ITERS, nr - 1)), dma((ITERS, nr - 1)),
            dma((ITERS + 1, nc - 1)), dma((ITERS + 1, nc - 1)),
            dma((ITERS + 1, nr - 1)), dma((ITERS + 1, nr - 1)),
            dma((ITERS - 1, nc - 1)), dma((ITERS - 1, nc - 1)),
            dma((ITERS - 1, nr - 1)), dma((ITERS - 1, nr - 1)),
        ],
        compiler_params=pltpu.CompilerParams(
            collective_id=0, has_side_effects=True, vmem_limit_bytes=48 << 20
        ),
    )(tab, keep, right_side, prior[None, :], blocks)


def solution(mesh):
    return jax.shard_map(
        shards,
        mesh=mesh,
        in_specs=(
            P("groups", ("row", "col")),
            P(("row", "col")),
            P(("row", "col"), None, None),
            P(("row", "col")),
            P(("row", "col")),
        ),
        out_specs=(P("groups", ("row", "col")), P("groups", ("row", "col"))),
        check_vma=False,
    )
```

```python
import functools

import jax
import jax.numpy as jnp
from jax import lax
from jax.experimental import pallas as pl
from jax.experimental.pallas import tpu as pltpu
from jax.sharding import PartitionSpec as P

BLOCK = 128
ITERS = 2
UNROLL = 16
PARTS = 2
MESH = pl.DeviceIdType.MESH
HIGHEST = lax.Precision.HIGHEST
f32 = jnp.float32
bf16 = jnp.bfloat16


def dot(left, right, dims):
    return lax.dot_general(
        left, right, (dims, ((), ())), precision=HIGHEST, preferred_element_type=f32
    )


def pair_gram(left, right):
    return dot(left, right, ((1,), (1,)))


def left_t(coeffs, panel):
    return dot(coeffs, panel, ((0,), (0,)))


def gauss_jordan(aug, frames):
    rows = lax.broadcasted_iota(jnp.int32, aug.shape, 0)
    for j in range(frames):
        at = frames + j
        lead = aug[j : j + 1, :] * (1.0 / aug[j : j + 1, at : at + 1])
        aug = jnp.where(rows == j, lead, aug - aug[:, at : at + 1] * lead)
    return aug[:, :frames]


def kernel(
    nr, nc, cb, kb, frames,
    tab_hbm, keep_hbm, rhs_hbm, prior_hbm, blocks_hbm, sol_ref, res_ref,
    tab, keep, rhs_ref, prior_ref,
    blocks, panels, feet, sendf, sendb, landf, landb, scan, image, direct, aug,
    gc0, gr0, gc1, gr1, gc2, gr2,
    in_sem, blk_sem, ag_s, ag_r, rs_s, rs_r, fg_s, fg_r, br_s, br_r, gc_s, gc_r, gr_s, gr_r,
    nc_s, nc_r, nr_s, nr_r,
):
    r = lax.axis_index("row")
    c = lax.axis_index("col")
    nrow, ncol = cb * nc, cb * nr
    half = frames // 2
    part = frames // PARTS
    span = lambda h: slice(h * part, (h + 1) * part)
    pending = []

    pairs = ((rhs_hbm, rhs_ref), (prior_hbm, prior_ref), (tab_hbm, tab), (keep_hbm, keep))
    loads = [
        pltpu.make_async_copy(src, dst, in_sem.at[i]) for i, (src, dst) in enumerate(pairs)
    ]
    loads.append(pltpu.make_async_copy(blocks_hbm, blocks, blk_sem))
    for load in loads:
        load.start()

    barrier = pltpu.get_barrier_semaphore()
    for axis, me, n in (("row", r, nr), ("col", c, nc)):
        for o in range(1, n):
            pl.semaphore_signal(
                barrier, inc=1, device_id={axis: lax.rem(me + o, n)}, device_id_type=MESH
            )

    def send(axis, me, n, src, dst, ssem, rsem):
        copies = []
        for o in range(1, n):
            peer = lax.rem(me + o, n)
            copy = pltpu.make_async_remote_copy(
                src_ref=src(peer), dst_ref=dst(o), send_sem=ssem.at[o - 1],
                recv_sem=rsem.at[o - 1], device_id={axis: peer}, device_id_type=MESH,
            )
            copy.start()
            copies.append(copy)
        pending.extend(copies)
        return copies

    def arrive(copies):
        for copy in copies:
            copy.wait_recv()

    def share(axis, me, n, buf, ssem, rsem, width=1):
        at = lambda _: buf.at[pl.ds(me * width, width)]
        return send(axis, me, n, at, at, ssem, rsem)

    def total(buf, n):
        out = buf[0]
        for i in range(1, n):
            out = out + buf[i]
        return out

    def fold(buf, me, gram):
        buf[me, :, :frames] = gram[:half]
        buf[me, :, frames:] = gram[half:]

    def unfold(packed):
        return jnp.concatenate([packed[:, :frames], packed[:, frames:]], axis=0)

    def put_panel(it, value):
        for h in range(PARTS):
            for b in range(cb):
                piece = value[span(h), b * BLOCK : (b + 1) * BLOCK]
                panels[h][it, r * cb + b] = piece.astype(bf16)

    def gather_rows(it):
        return [
            share("row", r, nr, panels[h].at[it], ag_s.at[it, h], ag_r.at[it, h], cb)
            for h in range(PARTS)
        ]

    def sweep(source, it, h, order_at, keep_at, side):
        def body(q, run):
            for u in range(UNROLL):
                t = q * UNROLL + u
                run = run * keep[keep_at + t] + lax.dot_general(
                    source[it, tab[order_at + kb + t]],
                    blocks[tab[order_at + t]],
                    (((1,), (side,)), ((), ())),
                    preferred_element_type=f32,
                )
                scan[h, t] = run
            return run

        lax.fori_loop(0, kb // UNROLL, body, jnp.zeros((part, BLOCK), f32))

    def segment(h, end_at, valid_at, i):
        return scan[h, tab[end_at + i]] * keep[valid_at + i]

    tab_c = 2 * kb + nrow
    keep_c = kb + nrow

    loads[0].wait()
    rhs = rhs_ref[...]
    put_panel(0, rhs)
    fold(gc0, c, pair_gram(rhs, rhs))
    pl.semaphore_wait(barrier, nr + nc - 2)

    gather = gather_rows(0)
    gram_cols = share("col", c, nc, gc0, gc_s.at[0], gc_r.at[0])
    gram = None
    for it in range(ITERS):
        last = it + 1 == ITERS
        now = rhs_ref if it == 0 else direct
        if it == 0:
            for load in loads[1:]:
                load.wait()
        copies = []
        for h in range(PARTS):
            arrive(gather[h])
            sweep(panels[h], it, h, 0, 0, 1)
            for i in range(nrow):
                sendf[it, h, i] = segment(h, 2 * kb, kb, i).astype(bf16)
            copies.append(send(
                "col", c, nc,
                lambda p: sendf.at[it, h, pl.ds(p * cb, cb)],
                lambda o: landf.at[it, h, o - 1],
                rs_s.at[it, h], rs_r.at[it, h],
            ))
        if it == 0:
            arrive(gram_cols)
            gr0[r] = total(gc0, nc)
            gram_rows = share("row", r, nr, gr0, gr_s.at[0], gr_r.at[0])
        direction = now[...]
        curvature = pair_gram(direction, prior_ref[...] * direction)
        spread = []
        for h in range(PARTS):
            arrive(copies[h])
            for b in range(cb):
                own = segment(h, 2 * kb, kb, c * cb + b)
                for o in range(1, nc):
                    own = own + landf[it, h, o - 1, b].astype(f32)
                feet[h][it, c * cb + b] = own.astype(bf16)
                image[span(h), b * BLOCK : (b + 1) * BLOCK] = own
            if h + 1 == PARTS:
                own = image[...]
                curvature = curvature + pair_gram(own, own.astype(bf16).astype(f32))
                fold(gc1.at[it], c, curvature)
                curve_cols = share(
                    "col", c, nc, gc1.at[it], gc_s.at[it + 1], gc_r.at[it + 1]
                )
            spread.append(
                share("col", c, nc, feet[h].at[it], fg_s.at[it, h], fg_r.at[it, h], cb)
            )
        copies = []
        for h in range(PARTS):
            arrive(spread[h])
            if h == 0:
                arrive(curve_cols)
                gr1[it, r] = total(gc1.at[it], nc)
                curve_rows = share(
                    "row", r, nr, gr1.at[it], gr_s.at[it + 1], gr_r.at[it + 1]
                )
            sweep(feet[h], it, h, tab_c, keep_c, 0)
            for i in range(ncol):
                sendb[it, h, i] = segment(h, tab_c + 2 * kb, keep_c + kb, i).astype(bf16)
            copies.append(send(
                "row", r, nr,
                lambda p: sendb.at[it, h, pl.ds(p * cb, cb)],
                lambda o: landb.at[it, h, o - 1],
                br_s.at[it, h], br_r.at[it, h],
            ))
        if it == 0:
            arrive(gram_rows)
            gram = unfold(total(gr0, nr))
        arrive(curve_rows)
        curvature = unfold(total(gr1.at[it], nr))
        aug[:, :frames] = gram
        aug[:, frames:] = 0.5 * (curvature + curvature.T)
        alpha = gauss_jordan(aug[...], frames)
        update = left_t(alpha, direction)
        sol_ref[...] = update if it == 0 else sol_ref[...] + update
        for h in range(PARTS):
            arrive(copies[h])
            for b in range(cb):
                at = slice(b * BLOCK, (b + 1) * BLOCK)
                own = segment(h, tab_c + 2 * kb, keep_c + kb, r * cb + b)
                for o in range(1, nr):
                    own = own + landb[it, h, o - 1, b].astype(f32)
                image[span(h), at] = own + prior_ref[:, at] * now[span(h), at]
        residual = (rhs_ref if it == 0 else res_ref)[...] - left_t(alpha, image[...])
        res_ref[...] = residual
        if not last:
            fold(gc2.at[it], c, pair_gram(residual, residual))
            arrive(share("col", c, nc, gc2.at[it], nc_s.at[it], nc_r.at[it]))
            gr2[it, r] = total(gc2.at[it], nc)
            gram_rows = share("row", r, nr, gr2.at[it], nr_s.at[it], nr_r.at[it])
            aug[:, frames:] = gram
            eye = lax.broadcasted_iota(jnp.int32, (frames, frames), 0)
            aug[:, :frames] = (
                eye == lax.broadcasted_iota(jnp.int32, (frames, frames), 1)
            ).astype(f32)
            gram_inverse = gauss_jordan(aug[...], frames)
            arrive(gram_rows)
            gram = unfold(total(gr2.at[it], nr))
            beta = dot(gram_inverse, gram, ((1,), (0,)))
            direct[...] = residual + left_t(beta, direction)
            put_panel(it + 1, direct)
            gather = gather_rows(it + 1)
    for copy in pending:
        copy.wait_send()


def order_by(key, other, count):
    kb = key.shape[0]
    ids = jnp.arange(kb, dtype=jnp.int32)
    full = key * kb + ids
    rank = jnp.sum((full[None, :] < full[:, None]).astype(jnp.int32), axis=1)
    onehot = (rank[None, :] == ids[:, None]).astype(jnp.int32)
    order = jnp.sum(onehot * ids[None, :], axis=1)
    picks = jnp.sum(onehot * other[None, :], axis=1)
    keys = jnp.sum(onehot * key[None, :], axis=1)
    keep = jnp.concatenate([jnp.zeros((1,), f32), (keys[1:] == keys[:-1]).astype(f32)])
    slots = jnp.arange(count, dtype=jnp.int32)[:, None]
    ends = jnp.maximum(jnp.sum((key[None, :] <= slots).astype(jnp.int32), axis=1) - 1, 0)
    valid = jnp.max((key[None, :] == slots).astype(f32), axis=1)
    return [order, picks, ends], [keep, valid]


def shards(right_side, prior, blocks, block_row, block_col):
    frames, pix = right_side.shape
    kb = blocks.shape[0]
    cb = pix // BLOCK
    nr = lax.axis_size("row")
    nc = lax.axis_size("col")
    nrow, ncol = cb * nc, cb * nr
    row_local = block_row % nrow
    col_local = block_col // nrow * cb + block_col % cb
    ints_r, keep_r = order_by(row_local, col_local, nrow)
    ints_c, keep_c = order_by(col_local, row_local, ncol)
    tab = jnp.concatenate(ints_r + ints_c)
    keep = jnp.concatenate(keep_r + keep_c)
    vm = pl.BlockSpec(memory_space=pltpu.VMEM)
    dma = pltpu.SemaphoreType.DMA
    tile = (frames // PARTS, BLOCK)
    pieces = (ITERS, PARTS)
    half = (frames // 2, 2 * frames)
    wide = (frames, 2 * frames)
    out = jax.ShapeDtypeStruct(right_side.shape, f32)
    return pl.pallas_call(
        functools.partial(kernel, nr, nc, cb, kb, frames),
        out_shape=(out, out),
        in_specs=[pl.BlockSpec(memory_space=pl.ANY)] * 5,
        out_specs=(vm, vm),
        scratch_shapes=[
            pltpu.SMEM(tab.shape, jnp.int32),
            pltpu.SMEM(keep.shape, f32),
            pltpu.VMEM(right_side.shape, f32),
            pltpu.VMEM((1, pix), f32),
            pltpu.VMEM(blocks.shape, bf16),
            [pltpu.VMEM((ITERS, ncol) + tile, bf16)] * PARTS,
            [pltpu.VMEM((ITERS, nrow) + tile, bf16)] * PARTS,
            pltpu.VMEM(pieces + (nrow,) + tile, bf16),
            pltpu.VMEM(pieces + (ncol,) + tile, bf16),
            pltpu.VMEM(pieces + (nc - 1, cb) + tile, bf16),
            pltpu.VMEM(pieces + (nr - 1, cb) + tile, bf16),
            pltpu.VMEM((PARTS, kb) + tile, f32),
            pltpu.VMEM(right_side.shape, f32),
            pltpu.VMEM(right_side.shape, f32),
            pltpu.VMEM(wide, f32),
            pltpu.VMEM((nc,) + half, f32),
            pltpu.VMEM((nr,) + half, f32),
            pltpu.VMEM((ITERS, nc) + half, f32),
            pltpu.VMEM((ITERS, nr) + half, f32),
            pltpu.VMEM((ITERS - 1, nc) + half, f32),
            pltpu.VMEM((ITERS - 1, nr) + half, f32),
            dma((4,)),
            dma,
            dma(pieces + (nr - 1,)), dma(pieces + (nr - 1,)),
            dma(pieces + (nc - 1,)), dma(pieces + (nc - 1,)),
            dma(pieces + (nc - 1,)), dma(pieces + (nc - 1,)),
            dma(pieces + (nr - 1,)), dma(pieces + (nr - 1,)),
            dma((ITERS + 1, nc - 1)), dma((ITERS + 1, nc - 1)),
            dma((ITERS + 1, nr - 1)), dma((ITERS + 1, nr - 1)),
            dma((ITERS - 1, nc - 1)), dma((ITERS - 1, nc - 1)),
            dma((ITERS - 1, nr - 1)), dma((ITERS - 1, nr - 1)),
        ],
        compiler_params=pltpu.CompilerParams(
            collective_id=0, has_side_effects=True, vmem_limit_bytes=48 << 20
        ),
    )(tab, keep, right_side, prior[None, :], blocks)


def solution(mesh):
    return jax.shard_map(
        shards,
        mesh=mesh,
        in_specs=(
            P("groups", ("row", "col")),
            P(("row", "col")),
            P(("row", "col"), None, None),
            P(("row", "col")),
            P(("row", "col")),
        ),
        out_specs=(P("groups", ("row", "col")), P("groups", ("row", "col"))),
        check_vma=False,
    )
```
